32 devices in a mesh: groups: 2 (over x), col: 16 (over z, y, core).
Axes of the slice: x: 2, y: 2, z: 4, core: 2. Of those that a mesh axis runs over, the one named last changes fastest.
Arguments:
- slab: float32 [2, 2048, 4096], P(None, 'groups', 'col'), parts along dimension 1, may hold values from -6 to 6
- block_on: int32 [16, 32], P('groups', 'col'), parts along dimension 0, may hold values 0 or 1
- block_band: int32 [16, 32], P('groups', 'col'), parts along dimension 0, may hold values from 0 to 3
- band_gain: float32 [4], replicated, may hold values from 0.25 to 2
Outputs:
- spectra: float32 [2, 2048, 4096], P(None, 'groups', 'col'), parts along dimension 1
The draws below stay inside these ranges and needn't reach their ends.
There are 2 independent parts, one for each index of `groups`. The reference program is written for one: setup_inputs(seed, part) draws one part's arguments, and reference() takes and returns one part's arrays. A program takes and returns all parts, laid end to end along the dimension named above; an argument that names none is the same for every part. Nothing has to cross between parts.
All inputs are finite; a program needn't handle non-finite values. No bound on the sum of `block_on` on one device may be relied on, other than what follows from the above.
Results may differ from the reference program's by a relative error of at most 0.00007.
Values sent between devices are 32-bit elements; how exact they have to be, the bound alone decides.
No kernel may reach another device: no remote copies, remote signals or barrier semaphores. Data moves between devices by JAX's collectives and lax.ppermute only.
A program may use at most 64 MiB of HBM per device.

```python
import math
import jax
import jax.numpy as jnp
from jax import lax

ROWS = 1024
BLOCK = 128
BANDS = 4
N = 4096
RB = 8
NKB = 32


def touch_ends(entries, stream_key, low, high):
    index_at = [jax.random.randint(jax.random.fold_in(stream_key, axis), (), 0, length) for axis, length in enumerate(entries.shape)]
    main_axis = entries.shape.index(max(entries.shape))
    beside = index_at[:main_axis] + [(index_at[main_axis] + 1) % entries.shape[main_axis]] + index_at[main_axis + 1:]
    return entries.at[tuple(index_at)].set(low).at[tuple(beside)].set(high)


def block_levels(stream_key, shape, cuts, low, high):
    gain, own = 1.0, jax.random.fold_in(stream_key, 6)
    for dim, blocks in cuts:
        steps = jnp.exp(jax.random.uniform(jax.random.fold_in(own, dim), (blocks,), jnp.float32, low / len(cuts), high / len(cuts)))
        gain = gain * jnp.repeat(steps, shape[dim] // blocks).reshape([-1 if axis == dim else 1 for axis in range(len(shape))])
    return gain


def normal_values(stream_key, dims, spread, limit, split=(), held_as=jnp.bfloat16):
    values = jax.random.normal(stream_key, dims, jnp.float32) * spread
    if len(split) > 0:
        values = block_levels(stream_key, dims, split, -0.22, 0.18) * values
    return jnp.clip(values, min=-limit, max=limit).astype(held_as)


def setup_inputs(seed: int = 0, part: int = 0) -> dict:
    splits = jax.random.split(jax.random.key(seed), 5)
    part_splits = jax.random.split(jax.random.fold_in(splits[4], part), 5)
    return {
        "slab": normal_values(part_splits[0], (2, ROWS, N), 1.0, 6.0, ((2, 16),), jnp.float32),
        "block_on": touch_ends((jax.random.randint(part_splits[1], (RB, NKB), 0, 2) < 1).astype(jnp.int32), jax.random.fold_in(part_splits[1], 1), 0, 1),
        "block_band": touch_ends(jax.random.randint(part_splits[2], (RB, NKB), 0, BANDS), jax.random.fold_in(part_splits[2], 1), 0, BANDS - 1).astype(jnp.int32),
        "band_gain": jnp.clip(jnp.exp(jax.random.uniform(splits[3], (BANDS,), jnp.float32, math.log(0.25), math.log(2.0))), 0.25, 2.0),
    }


def reference(slab, block_on, block_band, band_gain):
    signal = lax.complex(slab[0], slab[1])
    spectrum = jnp.fft.fft(signal, axis=-1, norm="ortho")
    stacked_parts = jnp.stack([jnp.real(spectrum), jnp.imag(spectrum)])
    selector = (block_band[..., None] == jnp.arange(BANDS, dtype=jnp.int32)).astype(band_gain.dtype)
    weights = block_on.astype(band_gain.dtype) * jnp.sum(selector * band_gain, axis=-1)
    shaped = stacked_parts.reshape(2, RB, BLOCK, NKB, BLOCK) * weights[None, :, None, :, None]
    return shaped.reshape(2, ROWS, N)
```

```python
import functools
import math

import jax
import jax.numpy as jnp
from jax import lax
from jax.experimental import pallas as pl
from jax.experimental.pallas import tpu as pltpu
from jax.sharding import PartitionSpec as P

BLOCK = 128
SUB = 8
LANES = 128


def phase_table(first_index, second_index, length):
    product = first_index[:, None] * second_index[None, :] % length
    angles = product.astype(jnp.float32) * (2.0 * math.pi / length)
    return (jnp.cos(angles), -jnp.sin(angles))


def contract(stacked, table, formula):
    cosine_table, sine_table = table
    ein = functools.partial(jnp.einsum, formula, precision=lax.Precision.HIGHEST)
    real_part = ein(stacked[0], cosine_table) - ein(stacked[1], sine_table)
    imag_part = ein(stacked[0], sine_table) + ein(stacked[1], cosine_table)
    return jnp.stack([real_part, imag_part])


def rotate(stacked, table):
    cosine_table, sine_table = table
    real_part = stacked[0] * cosine_table - stacked[1] * sine_table
    imag_part = stacked[0] * sine_table + stacked[1] * cosine_table
    return jnp.stack([real_part, imag_part])


def block_weights(block_on, block_band, band_gain, length):
    choose = (block_band[..., None] == jnp.arange(band_gain.shape[0], dtype=jnp.int32)).astype(
        jnp.float32
    )
    factor = 1.0 / math.sqrt(length)
    return block_on.astype(jnp.float32) * jnp.sum(choose * band_gain, axis=-1) * factor


def shards_generic(slab, block_on, block_band, band_gain):
    devices = lax.axis_size("col")
    rows_total, shard_cols = slab.shape[1:]
    length = shard_cols * devices
    rows_here = rows_total // devices
    first_len = BLOCK
    second_len = length // first_len
    first_iota = jnp.arange(first_len, dtype=jnp.int32)
    second_iota = jnp.arange(second_len, dtype=jnp.int32)
    table_one = phase_table(first_iota, first_iota, first_len)
    table_middle = phase_table(first_iota, second_iota, length)
    table_two = phase_table(second_iota, second_iota, second_len)
    received = lax.all_to_all(
        slab.reshape(2, devices, rows_here, shard_cols), "col", split_axis=1, concat_axis=3, tiled=True
    )
    square = received[:, 0].reshape(2, rows_here, first_len, second_len)
    mixture = rotate(contract(square, table_one, "rab,ak->rkb"), table_middle)
    whole = contract(mixture, table_two, "rkb,bm->rmk").reshape(2, rows_here, devices, shard_cols)
    spectrum = lax.all_to_all(whole, "col", split_axis=2, concat_axis=1, tiled=True)
    weight = block_weights(block_on, block_band, band_gain, length)
    blocked = spectrum.reshape(2, rows_total // BLOCK, BLOCK, shard_cols // BLOCK, BLOCK)
    return (blocked * weight[None, :, None, :, None]).reshape(2, rows_total, shard_cols)


def pack_rows_kernel(devices, slab_ref, mask_ref, out_ref):
    blocks = slab_ref.shape[1] // BLOCK
    halves = slab_ref.shape[2] // LANES

    @pl.loop(0, blocks)
    def _(block):
        for dev in range(devices):
            for plane in range(2):
                for half in range(halves):
                    out_ref[dev, (block * 2 + plane) * halves + half] = slab_ref[
                        plane, pl.ds(block * BLOCK + dev * SUB, SUB), half * LANES : (half + 1) * LANES
                    ]

    for dev in range(devices):
        out_ref[dev, blocks * 2 * halves] = mask_ref[...]


def butterflies(parts, length):
    if length == 1:
        return parts
    even = butterflies(parts[0::2], length // 2)
    odd = butterflies(parts[1::2], length // 2)
    low, high = [], []
    for index in range(length // 2):
        even_re, even_im = even[index]
        odd_re, odd_im = odd[index]
        if index == 0:
            turn_re, turn_im = odd_re, odd_im
        elif 4 * index == length:
            turn_re, turn_im = odd_im, -odd_re
        elif 8 * index == length:
            root = math.sqrt(0.5)
            turn_re, turn_im = (odd_re + odd_im) * root, (odd_im - odd_re) * root
        elif 8 * index == 3 * length:
            root = math.sqrt(0.5)
            turn_re, turn_im = (odd_im - odd_re) * root, (odd_re + odd_im) * -root
        else:
            angle = 2.0 * math.pi * index / length
            cosine, sine = math.cos(angle), math.sin(angle)
            turn_re = odd_re * cosine + odd_im * sine
            turn_im = odd_im * cosine - odd_re * sine
        low.append((even_re + turn_re, even_im + turn_im))
        high.append((even_re - turn_re, even_im - turn_im))
    return low + high


def transform_kernel(devices, x_ref, table_ref, twiddle_ref, out_ref, high_ref, low_ref, mid_ref):
    blocks = out_ref.shape[1] // 2
    halves = 2
    width = halves * LANES
    bits = devices.bit_length() - 1
    lane = lax.broadcasted_iota(jnp.int32, (2 * SUB, LANES), 1)

    @pl.loop(0, blocks // 2)
    def _(pair):
        for plane in range(2):
            for half in range(halves):
                vals = []
                for dev in range(devices):
                    tile0 = x_ref[dev, ((pair * 2) * 2 + plane) * halves + half]
                    tile1 = x_ref[dev, ((pair * 2 + 1) * 2 + plane) * halves + half]
                    vals.append(jnp.concatenate([tile0, tile1], axis=0))
                for bit in range(bits):
                    step = 1 << bit
                    odd_lane = (lane & step) != 0
                    for dev in range(devices):
                        if dev & step:
                            continue
                        first, second = vals[dev], vals[dev | step]
                        vals[dev] = jnp.where(odd_lane, pltpu.roll(second, step, 1), first)
                        vals[dev | step] = jnp.where(
                            odd_lane, second, pltpu.roll(first, LANES - step, 1)
                        )
                where = slice(plane * width + half * LANES, plane * width + (half + 1) * LANES)
                for dev in range(devices):
                    high = vals[dev].astype(jnp.bfloat16)
                    low = (vals[dev] - high.astype(jnp.float32)).astype(jnp.bfloat16)
                    high_ref[dev, pl.ds(pair * 2 * SUB, 2 * SUB), where] = high
                    low_ref[dev, pl.ds(pair * 2 * SUB, 2 * SUB), where] = low

    table = table_ref[...]
    table_high = table.astype(jnp.bfloat16)
    table_low = (table - table_high.astype(jnp.float32)).astype(jnp.bfloat16)
    rows = blocks * SUB
    group = 4

    for start in range(0, devices, group):
        lhs_high = high_ref[start : start + group].reshape(group * rows, 2 * width)
        lhs_low = low_ref[start : start + group].reshape(group * rows, 2 * width)
        dot = functools.partial(jnp.dot, preferred_element_type=jnp.float32)
        total = dot(lhs_high, table_high) + (dot(lhs_high, table_low) + dot(lhs_low, table_high))
        mid_ref[start : start + group] = total.reshape(group, rows, 2 * width)

    @pl.loop(0, blocks)
    def _(block):
        for half in range(halves):
            parts = []
            for dev in range(devices):
                re = mid_ref[dev, pl.ds(block * SUB, SUB), half * LANES : (half + 1) * LANES]
                im = mid_ref[
                    dev, pl.ds(block * SUB, SUB), width + half * LANES : width + (half + 1) * LANES
                ]
                if dev:
                    cosine = twiddle_ref[dev : dev + 1, half * LANES : (half + 1) * LANES]
                    sine = twiddle_ref[dev : dev + 1, width + half * LANES : width + (half + 1) * LANES]
                    re, im = re * cosine + im * sine, im * cosine - re * sine
                parts.append((re, im))
            for dev, (re, im) in enumerate(butterflies(parts, devices)):
                out_ref[dev, block * halves + half, 0] = re
                out_ref[dev, block * halves + half, 1] = im


def compact_kernel(devices, slots, index_ref, x_ref, out_ref):
    @pl.loop(0, devices)
    def _(dev):
        for slot in range(slots):
            out_ref[dev, slot] = x_ref[dev, index_ref[dev, slot]]


def spread_kernel(devices, slot_ref, weight_ref, x_ref, out_ref):
    halves = out_ref.shape[2] // LANES
    blocks = out_ref.shape[1] // BLOCK

    @pl.loop(0, blocks)
    def _(block):
        for half in range(halves):
            slot = slot_ref[block * halves + half]
            weight = weight_ref[block * halves + half]
            for dev in range(devices):
                for plane in range(2):
                    out_ref[
                        plane, pl.ds(block * BLOCK + dev * SUB, SUB), half * LANES : (half + 1) * LANES
                    ] = x_ref[dev, slot, plane] * weight


VMEM_SPEC = pl.BlockSpec(memory_space=pltpu.VMEM)
SMEM_SPEC = pl.BlockSpec(memory_space=pltpu.SMEM)


def shards_tiled(slab, block_on, block_band, band_gain):
    devices = lax.axis_size("col")
    rows_total, shard_cols = slab.shape[1:]
    length = shard_cols * devices
    blocks = rows_total // BLOCK
    halves = shard_cols // LANES
    tiles = blocks * halves
    width = shard_cols

    def call(body, out_shape, in_specs, scratch=(), name=None):
        return pl.pallas_call(
            body,
            out_shape=out_shape,
            in_specs=in_specs,
            out_specs=VMEM_SPEC,
            scratch_shapes=scratch,
            compiler_params=pltpu.CompilerParams(vmem_limit_bytes=32 << 20),
            name=name,
        )

    flags = jnp.zeros((SUB, LANES), jnp.float32)
    flags = flags.at[0, :tiles].set(block_on.reshape(tiles).astype(jnp.float32))
    message = call(
        functools.partial(pack_rows_kernel, devices),
        jax.ShapeDtypeStruct((devices, 2 * tiles + 1, SUB, LANES), jnp.float32),
        [VMEM_SPEC] * 2,
        name="pack_rows",
    )(slab, flags)
    received = lax.all_to_all(message, "col", split_axis=0, concat_axis=0, tiled=True)

    lane = jnp.arange(width, dtype=jnp.int32)
    point = (lane % devices) * (width // devices) + lane // devices
    cosine, minus_sine = phase_table(point, lane, width)
    table = jnp.concatenate(
        [
            jnp.concatenate([cosine, minus_sine], axis=1),
            jnp.concatenate([-minus_sine, cosine], axis=1),
        ],
        axis=0,
    )
    cosine, minus_sine = phase_table(jnp.arange(devices, dtype=jnp.int32), lane, length)
    twiddle = jnp.concatenate([cosine, -minus_sine], axis=1)

    spectrum = call(
        functools.partial(transform_kernel, devices),
        jax.ShapeDtypeStruct((devices, tiles, 2, SUB, LANES), jnp.float32),
        [VMEM_SPEC] * 3,
        [
            pltpu.VMEM((devices, blocks * SUB, 2 * width), jnp.bfloat16),
            pltpu.VMEM((devices, blocks * SUB, 2 * width), jnp.bfloat16),
            pltpu.VMEM((devices, blocks * SUB, 2 * width), jnp.float32),
        ],
        name="transform",
    )(received, table, twiddle)

    live = received[:, 2 * tiles, 0, :tiles] > 0.5
    tile_iota = jnp.arange(tiles, dtype=jnp.int32)
    before = tile_iota[None, :] < tile_iota[:, None]

    def slots_of(flag):
        rank = jnp.sum((flag[..., None, :] & before).astype(jnp.int32), axis=-1)
        return jnp.where(flag, rank, tiles)

    place = slots_of(live)
    match = place[:, None, :] == tile_iota[None, :, None]
    index = jnp.sum(jnp.where(match, tile_iota[None, None, :], 0), axis=-1)
    most = jnp.max(jnp.sum(live.astype(jnp.int32), axis=-1))

    own_place = slots_of(block_on.reshape(tiles) > 0)
    weight = block_weights(block_on, block_band, band_gain, length).reshape(tiles)

    def finish(capacity):
        def run(spectrum, index, own_place, weight):
            sent = call(
                functools.partial(compact_kernel, devices, capacity),
                jax.ShapeDtypeStruct((devices, capacity, 2, SUB, LANES), jnp.float32),
                [SMEM_SPEC, VMEM_SPEC],
                name="compact",
            )(index, spectrum)
            back = lax.all_to_all(sent, "col", split_axis=0, concat_axis=0, tiled=True)
            slot = jnp.minimum(own_place, capacity - 1)
            return call(
                functools.partial(spread_kernel, devices),
                jax.ShapeDtypeStruct(slab.shape, jnp.float32),
                [SMEM_SPEC, SMEM_SPEC, VMEM_SPEC],
                name="spread",
            )(slot, weight, back)

        return run

    capacities = sorted({max(1, tiles * part // 16) for part in (8, 10, 11, 12, 13, 14, 16)})
    bounds = jnp.array(capacities[:-1], jnp.int32)
    branch = jnp.sum((most > bounds).astype(jnp.int32))
    return lax.switch(branch, [finish(c) for c in capacities], spectrum, index, own_place, weight)


def shards(slab, block_on, block_band, band_gain):
    devices = lax.axis_size("col")
    rows_total, shard_cols = slab.shape[1:]
    power = devices & (devices - 1) == 0
    fits = (
        power
        and 2 <= devices <= 32
        and devices * SUB == BLOCK
        and shard_cols == 2 * LANES
        and rows_total % (2 * BLOCK) == 0
        and rows_total // BLOCK * 2 <= LANES
    )
    if fits:
        return shards_tiled(slab, block_on, block_band, band_gain)
    return shards_generic(slab, block_on, block_band, band_gain)


def solution(mesh):
    placed = (P(None, "groups", "col"), P("groups", "col"), P("groups", "col"), P())
    return jax.shard_map(
        shards, mesh=mesh, in_specs=placed, out_specs=P(None, "groups", "col"), check_vma=False
    )
```

```python
import functools
import math

import jax
import jax.numpy as jnp
from jax import lax
from jax.experimental import pallas as pl
from jax.experimental.pallas import tpu as pltpu
from jax.sharding import PartitionSpec as P

BLOCK = 128
SUB = 8
LANES = 128


def phase_table(first_index, second_index, length):
    product = first_index[:, None] * second_index[None, :] % length
    angles = product.astype(jnp.float32) * (2.0 * math.pi / length)
    return (jnp.cos(angles), -jnp.sin(angles))


def contract(stacked, table, formula):
    cosine_table, sine_table = table
    ein = functools.partial(jnp.einsum, formula, precision=lax.Precision.HIGHEST)
    real_part = ein(stacked[0], cosine_table) - ein(stacked[1], sine_table)
    imag_part = ein(stacked[0], sine_table) + ein(stacked[1], cosine_table)
    return jnp.stack([real_part, imag_part])


def rotate(stacked, table):
    cosine_table, sine_table = table
    real_part = stacked[0] * cosine_table - stacked[1] * sine_table
    imag_part = stacked[0] * sine_table + stacked[1] * cosine_table
    return jnp.stack([real_part, imag_part])


def block_weights(block_on, block_band, band_gain, length):
    choose = (block_band[..., None] == jnp.arange(band_gain.shape[0], dtype=jnp.int32)).astype(
        jnp.float32
    )
    factor = 1.0 / math.sqrt(length)
    return block_on.astype(jnp.float32) * jnp.sum(choose * band_gain, axis=-1) * factor


def shards_generic(slab, block_on, block_band, band_gain):
    devices = lax.axis_size("col")
    rows_total, shard_cols = slab.shape[1:]
    length = shard_cols * devices
    rows_here = rows_total // devices
    first_len = BLOCK
    second_len = length // first_len
    first_iota = jnp.arange(first_len, dtype=jnp.int32)
    second_iota = jnp.arange(second_len, dtype=jnp.int32)
    table_one = phase_table(first_iota, first_iota, first_len)
    table_middle = phase_table(first_iota, second_iota, length)
    table_two = phase_table(second_iota, second_iota, second_len)
    received = lax.all_to_all(
        slab.reshape(2, devices, rows_here, shard_cols), "col", split_axis=1, concat_axis=3, tiled=True
    )
    square = received[:, 0].reshape(2, rows_here, first_len, second_len)
    mixture = rotate(contract(square, table_one, "rab,ak->rkb"), table_middle)
    whole = contract(mixture, table_two, "rkb,bm->rmk").reshape(2, rows_here, devices, shard_cols)
    spectrum = lax.all_to_all(whole, "col", split_axis=2, concat_axis=1, tiled=True)
    weight = block_weights(block_on, block_band, band_gain, length)
    blocked = spectrum.reshape(2, rows_total // BLOCK, BLOCK, shard_cols // BLOCK, BLOCK)
    return (blocked * weight[None, :, None, :, None]).reshape(2, rows_total, shard_cols)


def travel_order(devices):
    return sorted(range(devices), key=lambda hop: (-hop.bit_length(), hop))


def pack_all_kernel(first, blocks, slab_ref, mask_ref, out_ref, sem):
    halves = slab_ref.shape[4] // LANES
    copies = []
    for plane in range(2):
        for block in range(blocks):
            for half in range(halves):
                copies.append(
                    pltpu.make_async_copy(
                        slab_ref.at[plane, first + block, :, :, half * LANES : (half + 1) * LANES],
                        out_ref.at[:, (plane * blocks + block) * halves + half],
                        sem.at[len(copies)],
                    )
                )
    for copy in copies:
        copy.start()
    for dev in range(out_ref.shape[0]):
        out_ref[dev, 2 * blocks * halves] = mask_ref[...]
    for copy in copies:
        copy.wait()


def pack_each_kernel(first, blocks, me_ref, slab_ref, *refs):
    outs, sem = refs[:-1], refs[-1]
    halves = slab_ref.shape[4] // LANES
    me = me_ref[0]
    copies = []
    for hop, out in zip(travel_order(len(outs)), outs):
        for half in range(halves):
            copies.append(
                pltpu.make_async_copy(
                    slab_ref.at[
                        :, first : first + blocks, me ^ hop, :, half * LANES : (half + 1) * LANES
                    ],
                    out.at[:, :, half],
                    sem.at[len(copies)],
                )
            )
    for copy in copies:
        copy.start()
    for copy in copies:
        copy.wait()


def butterflies(parts, length):
    if length == 1:
        return parts
    even = butterflies(parts[0::2], length // 2)
    odd = butterflies(parts[1::2], length // 2)
    low, high = [], []
    for index in range(length // 2):
        even_re, even_im = even[index]
        odd_re, odd_im = odd[index]
        if index == 0:
            turn_re, turn_im = odd_re, odd_im
        elif 4 * index == length:
            turn_re, turn_im = odd_im, -odd_re
        elif 8 * index == length:
            root = math.sqrt(0.5)
            turn_re, turn_im = (odd_re + odd_im) * root, (odd_im - odd_re) * root
        elif 8 * index == 3 * length:
            root = math.sqrt(0.5)
            turn_re, turn_im = (odd_im - odd_re) * root, (odd_re + odd_im) * -root
        else:
            angle = 2.0 * math.pi * index / length
            cosine, sine = math.cos(angle), math.sin(angle)
            turn_re = odd_re * cosine + odd_im * sine
            turn_im = odd_im * cosine - odd_re * sine
        low.append((even_re + turn_re, even_im + turn_im))
        high.append((even_re - turn_re, even_im - turn_im))
    return low + high


def transform_kernel(devices, blocks, table_ref, twiddle_ref, *refs):
    sources, (out_ref, high_ref, low_ref, mid_ref) = refs[:-4], refs[-4:]
    halves = 2
    width = halves * LANES
    bits = devices.bit_length() - 1
    lane = lax.broadcasted_iota(jnp.int32, (2 * SUB, LANES), 1)

    place = travel_order(devices)

    def tile_of(dev, plane, block, half):
        if len(sources) == 1:
            return sources[0][dev, (plane * blocks + block) * halves + half]
        return sources[place.index(dev)][plane, block, half]

    @pl.loop(0, blocks // 2)
    def _(pair):
        for plane in range(2):
            for half in range(halves):
                vals = [
                    jnp.concatenate(
                        [
                            tile_of(dev, plane, pair * 2, half),
                            tile_of(dev, plane, pair * 2 + 1, half),
                        ],
                        axis=0,
                    )
                    for dev in range(devices)
                ]
                for bit in range(bits):
                    step = 1 << bit
                    odd_lane = (lane & step) != 0
                    for dev in range(devices):
                        if dev & step:
                            continue
                        first, second = vals[dev], vals[dev | step]
                        vals[dev] = jnp.where(odd_lane, pltpu.roll(second, step, 1), first)
                        vals[dev | step] = jnp.where(
                            odd_lane, second, pltpu.roll(first, LANES - step, 1)
                        )
                where = slice(plane * width + half * LANES, plane * width + (half + 1) * LANES)
                for dev in range(devices):
                    high = vals[dev].astype(jnp.bfloat16)
                    low = (vals[dev] - high.astype(jnp.float32)).astype(jnp.bfloat16)
                    high_ref[dev, pl.ds(pair * 2 * SUB, 2 * SUB), where] = high
                    low_ref[dev, pl.ds(pair * 2 * SUB, 2 * SUB), where] = low

    table = table_ref[...]
    table_high = table.astype(jnp.bfloat16)
    table_low = (table - table_high.astype(jnp.float32)).astype(jnp.bfloat16)
    rows = blocks * SUB
    group = min(devices, 256 // rows)
    dot = functools.partial(jnp.dot, preferred_element_type=jnp.float32)
    for start in range(0, devices, group):
        lhs_high = high_ref[start : start + group].reshape(group * rows, 2 * width)
        lhs_low = low_ref[start : start + group].reshape(group * rows, 2 * width)
        total = dot(lhs_high, table_high) + (dot(lhs_high, table_low) + dot(lhs_low, table_high))
        mid_ref[start : start + group] = total.reshape(group, rows, 2 * width)

    @pl.loop(0, blocks)
    def _(block):
        for half in range(halves):
            parts = []
            for dev in range(devices):
                re = mid_ref[dev, pl.ds(block * SUB, SUB), half * LANES : (half + 1) * LANES]
                im = mid_ref[
                    dev, pl.ds(block * SUB, SUB), width + half * LANES : width + (half + 1) * LANES
                ]
                if dev:
                    cosine = twiddle_ref[dev : dev + 1, half * LANES : (half + 1) * LANES]
                    sine = twiddle_ref[dev : dev + 1, width + half * LANES : width + (half + 1) * LANES]
                    re, im = re * cosine + im * sine, im * cosine - re * sine
                parts.append((re, im))
            for dev, (re, im) in enumerate(butterflies(parts, devices)):
                out_ref[dev, block * halves + half, 0] = re
                out_ref[dev, block * halves + half, 1] = im


def compact_all_kernel(devices, slots, index_ref, x_ref, out_ref):
    @pl.loop(0, devices)
    def _(dev):
        for slot in range(slots):
            out_ref[dev, slot] = x_ref[dev, index_ref[dev, slot]]


def compact_each_kernel(devices, slots, me_ref, index_ref, first_ref, second_ref, *outs):
    split = first_ref.shape[1]
    me = me_ref[0]
    for hop, out in zip(travel_order(len(outs)), outs):
        dev = me ^ hop
        for slot in range(slots):
            index = index_ref[dev, slot]
            early = first_ref[dev, jnp.minimum(index, split - 1)]
            late = second_ref[dev, jnp.maximum(index - split, 0)]
            out[slot] = jnp.where(index < split, early, late)


def spread_kernel(devices, me_ref, slot_ref, weight_ref, first_ref, *refs):
    seconds, (out_ref, stage_ref, sem) = refs[:-3], refs[-3:]
    halves = out_ref.shape[2] // LANES
    blocks = out_ref.shape[1] // BLOCK
    split = first_ref.shape[1]
    last = seconds[0].shape[0] - 1
    me = me_ref[0]

    def copy_of(block):
        rows = pl.ds(pl.multiple_of(block * BLOCK, BLOCK), BLOCK)
        return pltpu.make_async_copy(stage_ref.at[:, rows], out_ref.at[:, rows], sem.at[block])

    @pl.loop(0, blocks)
    def _(block):
        for half in range(halves):
            slot = slot_ref[block * halves + half]
            weight = weight_ref[block * halves + half]
            early_slot = jnp.minimum(slot, split - 1)
            late_slot = jnp.clip(slot - split, 0, last)
            for number, hop in enumerate(travel_order(devices)):
                dev = me ^ hop
                row = pl.multiple_of(block * BLOCK + dev * SUB, SUB)
                tile = jnp.where(slot < split, first_ref[dev, early_slot], seconds[number][late_slot])
                for plane in range(2):
                    stage_ref[plane, pl.ds(row, SUB), half * LANES : (half + 1) * LANES] = (
                        tile[plane] * weight
                    )
        copy_of(block).start()

    @pl.loop(0, blocks)
    def _(block):
        copy_of(block).wait()


VMEM_SPEC = pl.BlockSpec(memory_space=pltpu.VMEM)
SMEM_SPEC = pl.BlockSpec(memory_space=pltpu.SMEM)
ANY_SPEC = pl.BlockSpec(memory_space=pl.ANY)


def shards_tiled(slab, block_on, block_band, band_gain):
    devices = lax.axis_size("col")
    rows_total, shard_cols = slab.shape[1:]
    length = shard_cols * devices
    blocks = rows_total // BLOCK
    halves = shard_cols // LANES
    tiles = blocks * halves
    width = shard_cols
    part = blocks // 2
    early = part * halves
    send_early = max(1, early // 2)
    me = lax.axis_index("col").astype(jnp.int32).reshape(1)

    def call(body, out_shape, in_specs, scratch=(), name=None, cost=None, out_spec=VMEM_SPEC, mib=12):
        many = isinstance(out_shape, list)
        return pl.pallas_call(
            body,
            out_shape=out_shape,
            in_specs=in_specs,
            out_specs=[out_spec] * len(out_shape) if many else out_spec,
            scratch_shapes=scratch,
            compiler_params=pltpu.CompilerParams(vmem_limit_bytes=mib << 20),
            cost_estimate=cost,
            name=name,
        )

    def trade(values):
        traded = []
        for hop, value in zip(travel_order(devices), values):
            pairs = [(dev, dev ^ hop) for dev in range(devices)]
            traded.append(lax.ppermute(value, "col", pairs) if hop else value)
        return traded

    def shape(*dims):
        return jax.ShapeDtypeStruct(dims, jnp.float32)

    dealt = slab.reshape(2, blocks, devices, SUB, shard_cols)
    flags = jnp.zeros((SUB, LANES), jnp.float32)
    flags = flags.at[0, :tiles].set(block_on.reshape(tiles).astype(jnp.float32))
    message = call(
        functools.partial(pack_all_kernel, 0, part),
        shape(devices, 2 * early + 1, SUB, LANES),
        [ANY_SPEC, VMEM_SPEC],
        [pltpu.SemaphoreType.DMA((2 * early,))],
        name="pack_all",
    )(dealt, flags)
    received = lax.all_to_all(message, "col", split_axis=0, concat_axis=0, tiled=True)
    pieces = call(
        functools.partial(pack_each_kernel, part, blocks - part),
        [shape(2, blocks - part, halves, SUB, LANES)] * devices,
        [SMEM_SPEC, ANY_SPEC],
        [pltpu.SemaphoreType.DMA((devices * halves,))],
        name="pack_each",
    )(me, dealt)
    arrived = trade(pieces)

    lane = jnp.arange(width, dtype=jnp.int32)

    def square(shift):
        point = ((lane % devices) ^ shift) * (width // devices) + lane // devices
        cosine, minus_sine = phase_table(point, lane, width)
        return jnp.concatenate(
            [
                jnp.concatenate([cosine, minus_sine], axis=1),
                jnp.concatenate([-minus_sine, cosine], axis=1),
            ],
            axis=0,
        )

    cosine, minus_sine = phase_table(jnp.arange(devices, dtype=jnp.int32), lane, length)
    twiddle = jnp.concatenate([cosine, -minus_sine], axis=1)

    def transform(count, table, sources):
        scratch = (devices, count * SUB, 2 * width)
        return call(
            functools.partial(transform_kernel, devices, count),
            shape(devices, count * halves, 2, SUB, LANES),
            [VMEM_SPEC] * (2 + len(sources)),
            [
                pltpu.VMEM(scratch, jnp.bfloat16),
                pltpu.VMEM(scratch, jnp.bfloat16),
                pltpu.VMEM(scratch, jnp.float32),
            ],
            name="transform",
            cost=pl.CostEstimate(
                flops=6 * devices * count * SUB * 4 * width * width,
                bytes_accessed=16 << 20,
                transcendentals=0,
            ),
        )(table, twiddle, *sources)

    live = received[:, 2 * early, 0, :tiles] > 0.5
    tile_iota = jnp.arange(tiles, dtype=jnp.int32)
    before = tile_iota[None, :] < tile_iota[:, None]
    is_early = tile_iota < early

    def slots_of(flag):
        rank = jnp.sum((flag[..., None, :] & before).astype(jnp.int32), axis=-1)
        ahead = jnp.sum((flag & is_early).astype(jnp.int32), axis=-1, keepdims=True)
        return rank + jnp.where(is_early, 0, jnp.maximum(send_early - ahead, 0))

    place = jnp.where(live, slots_of(live), 2 * tiles)
    slot_iota = jnp.arange(tiles + send_early, dtype=jnp.int32)
    match = place[:, None, :] == slot_iota[None, :, None]
    index = jnp.sum(jnp.where(match, tile_iota[None, None, :], 0), axis=-1)
    most = jnp.max(jnp.where(live, place - send_early + 1, 0))
    own_place = slots_of(block_on.reshape(tiles) > 0)
    weight = block_weights(block_on, block_band, band_gain, length).reshape(tiles)

    first = transform(part, square(0), [received])
    ahead = call(
        functools.partial(compact_all_kernel, devices, send_early),
        shape(devices, send_early, 2, SUB, LANES),
        [SMEM_SPEC, VMEM_SPEC],
        name="compact_all",
    )(index[:, :send_early], first)
    back = lax.all_to_all(ahead, "col", split_axis=0, concat_axis=0, tiled=True)
    second = transform(blocks - part, square(me[0]), arrived)

    def finish(capacity):
        def run(me, index, own_place, weight, first, second, back):
            sent = call(
                functools.partial(compact_each_kernel, devices, capacity),
                [shape(capacity, 2, SUB, LANES)] * devices,
                [SMEM_SPEC, SMEM_SPEC, VMEM_SPEC, VMEM_SPEC],
                name="compact_each",
            )(me, index[:, send_early : send_early + capacity], first, second)
            late = trade(sent)
            return call(
                functools.partial(spread_kernel, devices),
                shape(*slab.shape),
                [SMEM_SPEC] * 3 + [VMEM_SPEC] * (1 + devices),
                [pltpu.VMEM(slab.shape, jnp.float32), pltpu.SemaphoreType.DMA((blocks,))],
                name="spread",
                out_spec=ANY_SPEC,
            )(me, own_place, weight, back, *late)

        return run

    full = tiles - send_early
    capacities = sorted({max(1, full * step // 12) for step in (6, 7, 8, 9, 10, 12)})
    bounds = jnp.array(capacities[:-1], jnp.int32)
    branch = jnp.sum((most > bounds).astype(jnp.int32))
    return lax.switch(
        branch, [finish(c) for c in capacities], me, index, own_place, weight, first, second, back
    )


def shards(slab, block_on, block_band, band_gain):
    devices = lax.axis_size("col")
    rows_total, shard_cols = slab.shape[1:]
    power = devices & (devices - 1) == 0
    fits = (
        power
        and 2 <= devices <= 32
        and devices * SUB == BLOCK
        and shard_cols == 2 * LANES
        and rows_total % (4 * BLOCK) == 0
        and rows_total // BLOCK * 2 <= LANES
    )
    if fits:
        return shards_tiled(slab, block_on, block_band, band_gain)
    return shards_generic(slab, block_on, block_band, band_gain)


def solution(mesh):
    placed = (P(None, "groups", "col"), P("groups", "col"), P("groups", "col"), P())
    return jax.shard_map(
        shards, mesh=mesh, in_specs=placed, out_specs=P(None, "groups", "col"), check_vma=False
    )
```

```python
import functools
import math

import jax
import jax.numpy as jnp
from jax import lax
from jax.experimental import pallas as pl
from jax.experimental.pallas import tpu as pltpu
from jax.sharding import PartitionSpec as P


BLOCK = 128
SUB = 8
LANES = 128


def phase_table(first_index, second_index, length):
    product = first_index[:, None] * second_index[None, :] % length
    angles = product.astype(jnp.float32) * (2.0 * math.pi / length)
    return (jnp.cos(angles), -jnp.sin(angles))


def contract(stacked, table, formula):
    cosine_table, sine_table = table
    ein = functools.partial(jnp.einsum, formula, precision=lax.Precision.HIGHEST)
    real_part = ein(stacked[0], cosine_table) - ein(stacked[1], sine_table)
    imag_part = ein(stacked[0], sine_table) + ein(stacked[1], cosine_table)
    return jnp.stack([real_part, imag_part])


def rotate(stacked, table):
    cosine_table, sine_table = table
    real_part = stacked[0] * cosine_table - stacked[1] * sine_table
    imag_part = stacked[0] * sine_table + stacked[1] * cosine_table
    return jnp.stack([real_part, imag_part])


def block_weights(block_on, block_band, band_gain, length):
    choose = (block_band[..., None] == jnp.arange(band_gain.shape[0], dtype=jnp.int32)).astype(
        jnp.float32
    )
    factor = 1.0 / math.sqrt(length)
    return block_on.astype(jnp.float32) * jnp.sum(choose * band_gain, axis=-1) * factor


def shards_generic(slab, block_on, block_band, band_gain):
    devices = lax.axis_size("col")
    rows_total, shard_cols = slab.shape[1:]
    length = shard_cols * devices
    rows_here = rows_total // devices
    first_len = BLOCK
    second_len = length // first_len
    first_iota = jnp.arange(first_len, dtype=jnp.int32)
    second_iota = jnp.arange(second_len, dtype=jnp.int32)
    table_one = phase_table(first_iota, first_iota, first_len)
    table_middle = phase_table(first_iota, second_iota, length)
    table_two = phase_table(second_iota, second_iota, second_len)
    received = lax.all_to_all(
        slab.reshape(2, devices, rows_here, shard_cols), "col", split_axis=1, concat_axis=3, tiled=True
    )
    square = received[:, 0].reshape(2, rows_here, first_len, second_len)
    mixture = rotate(contract(square, table_one, "rab,ak->rkb"), table_middle)
    whole = contract(mixture, table_two, "rkb,bm->rmk").reshape(2, rows_here, devices, shard_cols)
    spectrum = lax.all_to_all(whole, "col", split_axis=2, concat_axis=1, tiled=True)
    weight = block_weights(block_on, block_band, band_gain, length)
    blocked = spectrum.reshape(2, rows_total // BLOCK, BLOCK, shard_cols // BLOCK, BLOCK)
    return (blocked * weight[None, :, None, :, None]).reshape(2, rows_total, shard_cols)


def travel_order(devices):
    return sorted(range(devices), key=lambda hop: (-hop.bit_length(), hop))


def pack_all_kernel(first, blocks, slab_ref, out_ref, sem):
    halves = slab_ref.shape[4] // LANES
    copies = []
    for plane in range(2):
        for block in range(blocks):
            for half in range(halves):
                copies.append(
                    pltpu.make_async_copy(
                        slab_ref.at[plane, first + block, :, :, half * LANES : (half + 1) * LANES],
                        out_ref.at[:, (plane * halves + half) * blocks + block],
                        sem.at[len(copies)],
                    )
                )
    for copy in copies:
        copy.start()
    for copy in copies:
        copy.wait()


def pack_each_kernel(first, blocks, me_ref, slab_ref, mask_ref, *refs):
    outs, (stage_ref, in_sem, out_sem) = refs[:-3], refs[-3:]
    halves = slab_ref.shape[4] // LANES
    me = me_ref[0]
    gathers, puts = [], []
    for number, hop in enumerate(travel_order(len(outs))):
        for plane in range(2):
            for half in range(halves):
                tile = (plane * halves + half) * blocks
                lanes = slice(half * LANES, (half + 1) * LANES)
                gathers.append(
                    pltpu.make_async_copy(
                        slab_ref.at[plane, first : first + blocks, me ^ hop, :, lanes],
                        stage_ref.at[number, tile : tile + blocks],
                        in_sem.at[len(gathers)],
                    )
                )
    for copy in gathers:
        copy.start()
    for number in range(len(outs)):
        stage_ref[number, 2 * halves * blocks] = mask_ref[...]
    for number, out in enumerate(outs):
        for copy in gathers[number * 2 * halves : (number + 1) * 2 * halves]:
            copy.wait()
        puts.append(pltpu.make_async_copy(stage_ref.at[number], out, out_sem.at[number]))
        puts[-1].start()
    for copy in puts:
        copy.wait()


def butterflies(parts, length):
    if length == 1:
        return parts
    even = butterflies(parts[0::2], length // 2)
    odd = butterflies(parts[1::2], length // 2)
    low, high = [], []
    for index in range(length // 2):
        even_re, even_im = even[index]
        odd_re, odd_im = odd[index]
        if index == 0:
            turn_re, turn_im = odd_re, odd_im
        elif 4 * index == length:
            turn_re, turn_im = odd_im, -odd_re
        elif 8 * index == length:
            root = math.sqrt(0.5)
            turn_re, turn_im = (odd_re + odd_im) * root, (odd_im - odd_re) * root
        elif 8 * index == 3 * length:
            root = math.sqrt(0.5)
            turn_re, turn_im = (odd_im - odd_re) * root, (odd_re + odd_im) * -root
        else:
            angle = 2.0 * math.pi * index / length
            cosine, sine = math.cos(angle), math.sin(angle)
            turn_re = odd_re * cosine + odd_im * sine
            turn_im = odd_im * cosine - odd_re * sine
        low.append((even_re + turn_re, even_im + turn_im))
        high.append((even_re - turn_re, even_im - turn_im))
    return low + high


def slots_kernel(tiles, bounds, sources, index_ref, place_ref, branch_ref):
    count = len(sources)
    flags = jnp.concatenate([source[source.shape[0] - 1, 0:1] for source in sources], axis=0)
    live = flags > 0.5
    lane = lax.broadcasted_iota(jnp.int32, (count, LANES), 1)
    row = lax.broadcasted_iota(jnp.int32, (LANES, LANES), 0)
    column = lax.broadcasted_iota(jnp.int32, (LANES, LANES), 1)
    ones = jnp.where(live, 1.0, 0.0)
    rank = jnp.dot(
        ones.astype(jnp.bfloat16),
        jnp.where(row < column, 1.0, 0.0).astype(jnp.bfloat16),
        preferred_element_type=jnp.float32,
    ).astype(jnp.int32)
    place = jnp.where(live, rank, LANES)
    index = jnp.zeros((count, LANES), jnp.int32)
    for tile in range(tiles):
        index = jnp.where(place[:, tile : tile + 1] == lane, tile, index)
    index_ref[...] = index
    place_ref[...] = rank
    most = jnp.max(jnp.sum(ones, axis=1, keepdims=True)).astype(jnp.int32)
    branch_ref[0] = sum((most > bound).astype(jnp.int32) for bound in bounds)


def transform_kernel(devices, blocks, masks, table_ref, twiddle_ref, *refs):
    sources, (high_ref, low_ref, mid_ref) = refs[: -7 if masks else -4], refs[-3:]
    out_ref = refs[len(sources)]
    if masks:
        slots_kernel(*masks, sources, *refs[len(sources) + 1 : len(sources) + 4])
    halves = 2
    width = halves * LANES
    bits = devices.bit_length() - 1
    lane = lax.broadcasted_iota(jnp.int32, (2 * SUB, LANES), 1)

    place = travel_order(devices)

    def tile_of(dev, plane, block, half):
        if len(sources) == 1:
            return sources[0][dev, (plane * halves + half) * blocks + block]
        return sources[place.index(dev)][(plane * halves + half) * blocks + block]

    @pl.loop(0, blocks // 2)
    def _(pair):
        for plane in range(2):
            for half in range(halves):
                vals = [
                    jnp.concatenate(
                        [
                            tile_of(dev, plane, pair * 2, half),
                            tile_of(dev, plane, pair * 2 + 1, half),
                        ],
                        axis=0,
                    )
                    for dev in range(devices)
                ]
                for bit in range(bits):
                    step = 1 << bit
                    odd_lane = (lane & step) != 0
                    for dev in range(devices):
                        if dev & step:
                            continue
                        first, second = vals[dev], vals[dev | step]
                        vals[dev] = jnp.where(odd_lane, pltpu.roll(second, step, 1), first)
                        vals[dev | step] = jnp.where(
                            odd_lane, second, pltpu.roll(first, LANES - step, 1)
                        )
                where = slice(plane * width + half * LANES, plane * width + (half + 1) * LANES)
                for dev in range(devices):
                    high = vals[dev].astype(jnp.bfloat16)
                    low = (vals[dev] - high.astype(jnp.float32)).astype(jnp.bfloat16)
                    high_ref[dev, pl.ds(pair * 2 * SUB, 2 * SUB), where] = high
                    low_ref[dev, pl.ds(pair * 2 * SUB, 2 * SUB), where] = low

    rows = blocks * SUB
    dot = functools.partial(jnp.dot, preferred_element_type=jnp.float32)
    lhs_high = high_ref[...].reshape(devices * rows, 2 * width)
    lhs_low = low_ref[...].reshape(devices * rows, 2 * width)
    for plane in range(2):
        columns = slice(plane * width, (plane + 1) * width)
        table = table_ref[:, columns]
        table_high = table.astype(jnp.bfloat16)
        table_low = (table - table_high.astype(jnp.float32)).astype(jnp.bfloat16)
        total = dot(lhs_high, table_high) + (dot(lhs_high, table_low) + dot(lhs_low, table_high))
        mid_ref[:, :, columns] = total.reshape(devices, rows, width)

    @pl.loop(0, blocks)
    def _(block):
        for half in range(halves):
            parts = []
            for dev in range(devices):
                re = mid_ref[dev, pl.ds(block * SUB, SUB), half * LANES : (half + 1) * LANES]
                im = mid_ref[
                    dev, pl.ds(block * SUB, SUB), width + half * LANES : width + (half + 1) * LANES
                ]
                if dev:
                    cosine = twiddle_ref[dev : dev + 1, half * LANES : (half + 1) * LANES]
                    sine = twiddle_ref[dev : dev + 1, width + half * LANES : width + (half + 1) * LANES]
                    re, im = re * cosine + im * sine, im * cosine - re * sine
                parts.append((re, im))
            for dev, (re, im) in enumerate(butterflies(parts, devices)):
                out_ref[dev, block * halves + half, 0] = re
                out_ref[dev, block * halves + half, 1] = im


def compact_kernel(slots, me_ref, index_ref, first_ref, second_ref, *outs):
    split = first_ref.shape[1]
    me = me_ref[0]
    for number, (hop, out) in enumerate(zip(travel_order(len(outs)), outs)):
        dev = me ^ hop
        for slot in range(slots):
            index = index_ref[number, slot]
            early = first_ref[dev, jnp.minimum(index, split - 1)]
            late = second_ref[dev, jnp.maximum(index - split, 0)]
            out[slot] = jnp.where(index < split, early, late)


def spread_kernel(devices, me_ref, slot_ref, weight_ref, *refs):
    sources, (out_ref, stage_ref, sem) = refs[:-3], refs[-3:]
    halves = out_ref.shape[2] // LANES
    blocks = out_ref.shape[1] // BLOCK
    last = sources[0].shape[0] - 1
    me = me_ref[0]

    def copy_of(block):
        rows = pl.ds(pl.multiple_of(block * BLOCK, BLOCK), BLOCK)
        return pltpu.make_async_copy(stage_ref.at[:, rows], out_ref.at[:, rows], sem.at[block])

    @pl.loop(0, blocks)
    def _(block):
        for half in range(halves):
            slot = jnp.minimum(slot_ref[block * halves + half], last)
            weight = weight_ref[block * halves + half]
            for number, hop in enumerate(travel_order(devices)):
                row = pl.multiple_of(block * BLOCK + (me ^ hop) * SUB, SUB)
                for plane in range(2):
                    stage_ref[plane, pl.ds(row, SUB), half * LANES : (half + 1) * LANES] = (
                        sources[number][slot, plane] * weight
                    )
        copy_of(block).start()

    @pl.loop(0, blocks)
    def _(block):
        copy_of(block).wait()


VMEM_SPEC = pl.BlockSpec(memory_space=pltpu.VMEM)
SMEM_SPEC = pl.BlockSpec(memory_space=pltpu.SMEM)
ANY_SPEC = pl.BlockSpec(memory_space=pl.ANY)
HBM_SPEC = pl.BlockSpec(memory_space=pltpu.HBM)
PIECE_SPEC = HBM_SPEC


def shards_tiled(slab, block_on, block_band, band_gain):
    devices = lax.axis_size("col")
    rows_total, shard_cols = slab.shape[1:]
    length = shard_cols * devices
    blocks = rows_total // BLOCK
    halves = shard_cols // LANES
    tiles = blocks * halves
    width = shard_cols
    part = blocks * 3 // 4
    early = part * halves
    me = lax.axis_index("col").astype(jnp.int32).reshape(1)

    def call(body, out_shape, in_specs, scratch=(), cost=None, out_spec=VMEM_SPEC, mib=14):
        many = isinstance(out_shape, list)
        return pl.pallas_call(
            body,
            out_shape=out_shape,
            in_specs=in_specs,
            out_specs=[
                SMEM_SPEC if out.shape == (1,) else out_spec for out in out_shape
            ]
            if many
            else out_spec,
            scratch_shapes=scratch,
            compiler_params=pltpu.CompilerParams(vmem_limit_bytes=mib << 20),
            cost_estimate=cost,
        )

    def trade(values):
        traded = []
        for hop, value in zip(travel_order(devices), values):
            pairs = [(dev, dev ^ hop) for dev in range(devices)]
            traded.append(lax.ppermute(value, "col", pairs) if hop else value)
        return traded

    def shape(*dims):
        return jax.ShapeDtypeStruct(dims, jnp.float32)

    dealt = slab.reshape(2, blocks, devices, SUB, shard_cols)
    flags = jnp.zeros((SUB, LANES), jnp.float32)
    flags = flags.at[0, :tiles].set(block_on.reshape(tiles).astype(jnp.float32))
    pieces = call(
        functools.partial(pack_each_kernel, 0, part),
        [shape(2 * early + 1, SUB, LANES)] * devices,
        [SMEM_SPEC, HBM_SPEC, VMEM_SPEC],
        [
            pltpu.VMEM((devices, 2 * early + 1, SUB, LANES), jnp.float32),
            pltpu.SemaphoreType.DMA((devices * 2 * halves,)),
            pltpu.SemaphoreType.DMA((devices,)),
        ],
        out_spec=PIECE_SPEC,
    )(me, dealt, flags)
    arrived = trade(pieces)
    message = call(
        functools.partial(pack_all_kernel, part, blocks - part),
        shape(devices, 2 * (tiles - early), SUB, LANES),
        [HBM_SPEC],
        [pltpu.SemaphoreType.DMA((2 * (tiles - early),))],
    )(dealt)
    received = lax.all_to_all(message, "col", split_axis=0, concat_axis=0, tiled=True)

    lane = jnp.arange(width, dtype=jnp.int32)

    def square(shift):
        point = ((lane % devices) ^ shift) * (width // devices) + lane // devices
        cosine, minus_sine = phase_table(point, lane, width)
        return jnp.concatenate(
            [
                jnp.concatenate([cosine, minus_sine], axis=1),
                jnp.concatenate([-minus_sine, cosine], axis=1),
            ],
            axis=0,
        )

    cosine, minus_sine = phase_table(jnp.arange(devices, dtype=jnp.int32), lane, length)
    twiddle = jnp.concatenate([cosine, -minus_sine], axis=1)

    capacities = sorted({max(1, tiles * step // 16) for step in (8, 10, 11, 12, 13, 14, 16)})

    def transform(count, masks, table, sources):
        scratch = (devices, count * SUB, 2 * width)
        outs = [shape(devices, count * halves, 2, SUB, LANES)]
        if masks:
            outs += [
                jax.ShapeDtypeStruct((devices, LANES), jnp.int32),
                jax.ShapeDtypeStruct((devices, LANES), jnp.int32),
                jax.ShapeDtypeStruct((1,), jnp.int32),
            ]
        return call(
            functools.partial(transform_kernel, devices, count, masks),
            outs,
            [VMEM_SPEC] * (2 + len(sources)),
            [
                pltpu.VMEM(scratch, jnp.bfloat16),
                pltpu.VMEM(scratch, jnp.bfloat16),
                pltpu.VMEM(scratch, jnp.float32),
            ],
            cost=pl.CostEstimate(
                flops=6 * devices * count * SUB * 4 * width * width,
                bytes_accessed=16 << 20,
                transcendentals=0,
            ),
        )(table, twiddle, *sources)

    weight = block_weights(block_on, block_band, band_gain, length).reshape(tiles)

    first, index, place, branch = transform(part, (tiles, capacities[:-1]), square(me[0]), arrived)
    own_place = place[devices - 1, :tiles]
    (second,) = transform(blocks - part, (), square(0), [received])

    def finish(capacity):
        def run(me, index, own_place, weight, first, second):
            sent = call(
                functools.partial(compact_kernel, capacity),
                [shape(capacity, 2, SUB, LANES)] * devices,
                [SMEM_SPEC, SMEM_SPEC, VMEM_SPEC, VMEM_SPEC],
            )(me, index, first, second)
            return call(
                functools.partial(spread_kernel, devices),
                shape(*slab.shape),
                [SMEM_SPEC] * 3 + [VMEM_SPEC] * devices,
                [pltpu.VMEM(slab.shape, jnp.float32), pltpu.SemaphoreType.DMA((blocks,))],
                out_spec=HBM_SPEC,
            )(me, own_place, weight, *trade(sent))

        return run

    branches = [finish(c) for c in capacities]
    return branch[0], branches, (me, index, own_place, weight, first, second)


def shards(slab, block_on, block_band, band_gain):
    devices = lax.axis_size("col")
    rows_total, shard_cols = slab.shape[1:]
    power = devices & (devices - 1) == 0
    fits = (
        power
        and 2 <= devices <= 32
        and devices * SUB == BLOCK
        and shard_cols == 2 * LANES
        and rows_total % (4 * BLOCK) == 0
        and rows_total // BLOCK * 2 <= LANES
    )
    if fits:
        branch, branches, operands = shards_tiled(slab, block_on, block_band, band_gain)
        return lax.switch(branch, branches, *operands)
    return shards_generic(slab, block_on, block_band, band_gain)


def solution(mesh):
    placed = (P(None, "groups", "col"), P("groups", "col"), P("groups", "col"), P())
    return jax.shard_map(
        shards, mesh=mesh, in_specs=placed, out_specs=P(None, "groups", "col"), check_vma=False
    )
```

```python
import functools
import math

import jax
import jax.numpy as jnp
from jax import lax
from jax.experimental import pallas as pl
from jax.experimental.pallas import tpu as pltpu
from jax.sharding import PartitionSpec as P


BLOCK = 128
SUB = 8
LANES = 128


def phase_table(first_index, second_index, length):
    product = first_index[:, None] * second_index[None, :] % length
    angles = product.astype(jnp.float32) * (2.0 * math.pi / length)
    return (jnp.cos(angles), -jnp.sin(angles))


def contract(stacked, table, formula):
    cosine_table, sine_table = table
    ein = functools.partial(jnp.einsum, formula, precision=lax.Precision.HIGHEST)
    real_part = ein(stacked[0], cosine_table) - ein(stacked[1], sine_table)
    imag_part = ein(stacked[0], sine_table) + ein(stacked[1], cosine_table)
    return jnp.stack([real_part, imag_part])


def rotate(stacked, table):
    cosine_table, sine_table = table
    real_part = stacked[0] * cosine_table - stacked[1] * sine_table
    imag_part = stacked[0] * sine_table + stacked[1] * cosine_table
    return jnp.stack([real_part, imag_part])


def block_weights(block_on, block_band, band_gain, length):
    choose = (block_band[..., None] == jnp.arange(band_gain.shape[0], dtype=jnp.int32)).astype(
        jnp.float32
    )
    factor = 1.0 / math.sqrt(length)
    return block_on.astype(jnp.float32) * jnp.sum(choose * band_gain, axis=-1) * factor


def shards_generic(slab, block_on, block_band, band_gain):
    devices = lax.axis_size("col")
    rows_total, shard_cols = slab.shape[1:]
    length = shard_cols * devices
    rows_here = rows_total // devices
    first_len = BLOCK
    second_len = length // first_len
    first_iota = jnp.arange(first_len, dtype=jnp.int32)
    second_iota = jnp.arange(second_len, dtype=jnp.int32)
    table_one = phase_table(first_iota, first_iota, first_len)
    table_middle = phase_table(first_iota, second_iota, length)
    table_two = phase_table(second_iota, second_iota, second_len)
    received = lax.all_to_all(
        slab.reshape(2, devices, rows_here, shard_cols), "col", split_axis=1, concat_axis=3, tiled=True
    )
    square = received[:, 0].reshape(2, rows_here, first_len, second_len)
    mixture = rotate(contract(square, table_one, "rab,ak->rkb"), table_middle)
    whole = contract(mixture, table_two, "rkb,bm->rmk").reshape(2, rows_here, devices, shard_cols)
    spectrum = lax.all_to_all(whole, "col", split_axis=2, concat_axis=1, tiled=True)
    weight = block_weights(block_on, block_band, band_gain, length)
    blocked = spectrum.reshape(2, rows_total // BLOCK, BLOCK, shard_cols // BLOCK, BLOCK)
    return (blocked * weight[None, :, None, :, None]).reshape(2, rows_total, shard_cols)


def travel_order(devices):
    return sorted(range(devices), key=lambda hop: (-hop.bit_length(), hop))


def pack_all_kernel(first, blocks, slab_ref, out_ref, sem):
    halves = slab_ref.shape[4] // LANES
    copies = []
    for plane in range(2):
        for block in range(blocks):
            for half in range(halves):
                copies.append(
                    pltpu.make_async_copy(
                        slab_ref.at[plane, first + block, :, :, half * LANES : (half + 1) * LANES],
                        out_ref.at[:, (plane * halves + half) * blocks + block],
                        sem.at[len(copies)],
                    )
                )
    for copy in copies:
        copy.start()
    for copy in copies:
        copy.wait()


def pack_each_kernel(first, blocks, me_ref, slab_ref, mask_ref, *refs):
    outs, sem = refs[:-1], refs[-1]
    halves = slab_ref.shape[4] // LANES
    me = me_ref[0]
    copies = []
    for hop, out in zip(travel_order(len(outs)), outs):
        for plane in range(2):
            for half in range(halves):
                tile = (plane * halves + half) * blocks
                lanes = slice(half * LANES, (half + 1) * LANES)
                copies.append(
                    pltpu.make_async_copy(
                        slab_ref.at[plane, first : first + blocks, me ^ hop, :, lanes],
                        out.at[tile : tile + blocks],
                        sem.at[len(copies)],
                    )
                )
        copies.append(
            pltpu.make_async_copy(mask_ref, out.at[2 * halves * blocks], sem.at[len(copies)])
        )
    for copy in copies:
        copy.start()
    for copy in copies:
        copy.wait()


def butterflies(parts, length):
    if length == 1:
        return parts
    even = butterflies(parts[0::2], length // 2)
    odd = butterflies(parts[1::2], length // 2)
    low, high = [], []
    for index in range(length // 2):
        even_re, even_im = even[index]
        odd_re, odd_im = odd[index]
        if index == 0:
            turn_re, turn_im = odd_re, odd_im
        elif 4 * index == length:
            turn_re, turn_im = odd_im, -odd_re
        elif 8 * index == length:
            root = math.sqrt(0.5)
            turn_re, turn_im = (odd_re + odd_im) * root, (odd_im - odd_re) * root
        elif 8 * index == 3 * length:
            root = math.sqrt(0.5)
            turn_re, turn_im = (odd_im - odd_re) * root, (odd_re + odd_im) * -root
        else:
            angle = 2.0 * math.pi * index / length
            cosine, sine = math.cos(angle), math.sin(angle)
            turn_re = odd_re * cosine + odd_im * sine
            turn_im = odd_im * cosine - odd_re * sine
        low.append((even_re + turn_re, even_im + turn_im))
        high.append((even_re - turn_re, even_im - turn_im))
    return low + high


def slots_kernel(tiles, bounds, sources, index_ref, place_ref, branch_ref):
    count = len(sources)
    flags = jnp.concatenate([source[source.shape[0] - 1, 0:1] for source in sources], axis=0)
    live = flags > 0.5
    lane = lax.broadcasted_iota(jnp.int32, (count, LANES), 1)
    row = lax.broadcasted_iota(jnp.int32, (LANES, LANES), 0)
    column = lax.broadcasted_iota(jnp.int32, (LANES, LANES), 1)
    ones = jnp.where(live, 1.0, 0.0)
    rank = jnp.dot(
        ones.astype(jnp.bfloat16),
        jnp.where(row < column, 1.0, 0.0).astype(jnp.bfloat16),
        preferred_element_type=jnp.float32,
    ).astype(jnp.int32)
    place = jnp.where(live, rank, LANES)
    index = jnp.zeros((count, LANES), jnp.int32)
    for tile in range(tiles):
        index = jnp.where(place[:, tile : tile + 1] == lane, tile, index)
    index_ref[...] = index
    place_ref[...] = rank
    most = jnp.max(jnp.sum(ones, axis=1, keepdims=True)).astype(jnp.int32)
    branch_ref[0] = sum((most > bound).astype(jnp.int32) for bound in bounds)


def transform_kernel(devices, blocks, masks, table_ref, twiddle_ref, *refs):
    sources, (high_ref, low_ref, mid_ref) = refs[: -7 if masks else -4], refs[-3:]
    out_ref = refs[len(sources)]
    if masks:
        slots_kernel(*masks, sources, *refs[len(sources) + 1 : len(sources) + 4])
    halves = 2
    width = halves * LANES
    bits = devices.bit_length() - 1
    lane = lax.broadcasted_iota(jnp.int32, (2 * SUB, LANES), 1)

    place = travel_order(devices)

    def tile_of(dev, plane, block, half):
        if len(sources) == 1:
            return sources[0][dev, (plane * halves + half) * blocks + block]
        return sources[place.index(dev)][(plane * halves + half) * blocks + block]

    @pl.loop(0, blocks // 2)
    def _(pair):
        for plane in range(2):
            for half in range(halves):
                vals = [
                    jnp.concatenate(
                        [
                            tile_of(dev, plane, pair * 2, half),
                            tile_of(dev, plane, pair * 2 + 1, half),
                        ],
                        axis=0,
                    )
                    for dev in range(devices)
                ]
                for bit in range(bits):
                    step = 1 << bit
                    odd_lane = (lane & step) != 0
                    for dev in range(devices):
                        if dev & step:
                            continue
                        first, second = vals[dev], vals[dev | step]
                        moved = jnp.take_along_axis(
                            jnp.where(odd_lane, first, second), lane ^ step, axis=1
                        )
                        vals[dev] = jnp.where(odd_lane, moved, first)
                        vals[dev | step] = jnp.where(odd_lane, second, moved)
                where = slice(plane * width + half * LANES, plane * width + (half + 1) * LANES)
                for dev in range(devices):
                    high = vals[dev].astype(jnp.bfloat16)
                    low = (vals[dev] - high.astype(jnp.float32)).astype(jnp.bfloat16)
                    high_ref[dev, pl.ds(pair * 2 * SUB, 2 * SUB), where] = high
                    low_ref[dev, pl.ds(pair * 2 * SUB, 2 * SUB), where] = low

    rows = blocks * SUB
    dot = functools.partial(jnp.dot, preferred_element_type=jnp.float32)
    lhs_high = high_ref[...].reshape(devices * rows, 2 * width)
    lhs_low = low_ref[...].reshape(devices * rows, 2 * width)
    for plane in range(2):
        columns = slice(plane * width, (plane + 1) * width)
        table = table_ref[:, columns]
        table_high = table.astype(jnp.bfloat16)
        table_low = (table - table_high.astype(jnp.float32)).astype(jnp.bfloat16)
        total = dot(lhs_high, table_high) + (dot(lhs_high, table_low) + dot(lhs_low, table_high))
        mid_ref[:, :, columns] = total.reshape(devices, rows, width)

    @pl.loop(0, blocks)
    def _(block):
        for half in range(halves):
            parts = []
            for dev in range(devices):
                re = mid_ref[dev, pl.ds(block * SUB, SUB), half * LANES : (half + 1) * LANES]
                im = mid_ref[
                    dev, pl.ds(block * SUB, SUB), width + half * LANES : width + (half + 1) * LANES
                ]
                if dev:
                    cosine = twiddle_ref[dev : dev + 1, half * LANES : (half + 1) * LANES]
                    sine = twiddle_ref[dev : dev + 1, width + half * LANES : width + (half + 1) * LANES]
                    re, im = re * cosine + im * sine, im * cosine - re * sine
                parts.append((re, im))
            for dev, (re, im) in enumerate(butterflies(parts, devices)):
                out_ref[dev, block * halves + half, 0] = re
                out_ref[dev, block * halves + half, 1] = im


def compact_kernel(slots, me_ref, index_ref, first_ref, second_ref, *outs):
    split = first_ref.shape[1]
    me = me_ref[0]
    for number, (hop, out) in enumerate(zip(travel_order(len(outs)), outs)):
        dev = me ^ hop
        for slot in range(slots):
            index = index_ref[number, slot]
            early = first_ref[dev, jnp.minimum(index, split - 1)]
            late = second_ref[dev, jnp.maximum(index - split, 0)]
            out[slot] = jnp.where(index < split, early, late)


def spread_kernel(devices, me_ref, slot_ref, weight_ref, *refs):
    sources, (out_ref, stage_ref, sem) = refs[:-3], refs[-3:]
    halves = out_ref.shape[2] // LANES
    blocks = out_ref.shape[1] // BLOCK
    last = sources[0].shape[0] - 1
    me = me_ref[0]

    def copy_of(block):
        rows = pl.ds(pl.multiple_of(block * BLOCK, BLOCK), BLOCK)
        return pltpu.make_async_copy(stage_ref.at[:, rows], out_ref.at[:, rows], sem.at[block])

    @pl.loop(0, blocks)
    def _(block):
        for half in range(halves):
            slot = jnp.minimum(slot_ref[block * halves + half], last)
            weight = weight_ref[block * halves + half]
            for number, hop in enumerate(travel_order(devices)):
                row = pl.multiple_of(block * BLOCK + (me ^ hop) * SUB, SUB)
                for plane in range(2):
                    stage_ref[plane, pl.ds(row, SUB), half * LANES : (half + 1) * LANES] = (
                        sources[number][slot, plane] * weight
                    )
        copy_of(block).start()

    @pl.loop(0, blocks)
    def _(block):
        copy_of(block).wait()


VMEM_SPEC = pl.BlockSpec(memory_space=pltpu.VMEM)
SMEM_SPEC = pl.BlockSpec(memory_space=pltpu.SMEM)
ANY_SPEC = pl.BlockSpec(memory_space=pl.ANY)
HBM_SPEC = pl.BlockSpec(memory_space=pltpu.HBM)
PIECE_SPEC = HBM_SPEC


def shards_tiled(slab, block_on, block_band, band_gain):
    devices = lax.axis_size("col")
    rows_total, shard_cols = slab.shape[1:]
    length = shard_cols * devices
    blocks = rows_total // BLOCK
    halves = shard_cols // LANES
    tiles = blocks * halves
    width = shard_cols
    part = blocks * 3 // 4
    early = part * halves
    me = lax.axis_index("col").astype(jnp.int32).reshape(1)

    def call(body, out_shape, in_specs, scratch=(), cost=None, out_spec=VMEM_SPEC, mib=14):
        many = isinstance(out_shape, list)
        return pl.pallas_call(
            body,
            out_shape=out_shape,
            in_specs=in_specs,
            out_specs=[
                SMEM_SPEC if out.shape == (1,) else out_spec for out in out_shape
            ]
            if many
            else out_spec,
            scratch_shapes=scratch,
            compiler_params=pltpu.CompilerParams(vmem_limit_bytes=mib << 20),
            cost_estimate=cost,
        )

    def trade(values):
        traded = []
        for hop, value in zip(travel_order(devices), values):
            pairs = [(dev, dev ^ hop) for dev in range(devices)]
            traded.append(lax.ppermute(value, "col", pairs) if hop else value)
        return traded

    def shape(*dims):
        return jax.ShapeDtypeStruct(dims, jnp.float32)

    dealt = slab.reshape(2, blocks, devices, SUB, shard_cols)
    flags = jnp.zeros((SUB, LANES), jnp.float32)
    flags = flags.at[0, :tiles].set(block_on.reshape(tiles).astype(jnp.float32))
    pieces = call(
        functools.partial(pack_each_kernel, 0, part),
        [shape(2 * early + 1, SUB, LANES)] * devices,
        [SMEM_SPEC, VMEM_SPEC, VMEM_SPEC],
        [pltpu.SemaphoreType.DMA((devices * (2 * halves + 1),))],
        out_spec=PIECE_SPEC,
    )(me, dealt, flags)
    arrived = trade(pieces)
    message = call(
        functools.partial(pack_all_kernel, part, blocks - part),
        shape(devices, 2 * (tiles - early), SUB, LANES),
        [VMEM_SPEC],
        [pltpu.SemaphoreType.DMA((2 * (tiles - early),))],
    )(dealt)
    received = lax.all_to_all(message, "col", split_axis=0, concat_axis=0, tiled=True)

    lane = jnp.arange(width, dtype=jnp.int32)

    def square(shift):
        point = ((lane % devices) ^ shift) * (width // devices) + lane // devices
        cosine, minus_sine = phase_table(point, lane, width)
        return jnp.concatenate(
            [
                jnp.concatenate([cosine, minus_sine], axis=1),
                jnp.concatenate([-minus_sine, cosine], axis=1),
            ],
            axis=0,
        )

    cosine, minus_sine = phase_table(jnp.arange(devices, dtype=jnp.int32), lane, length)
    twiddle = jnp.concatenate([cosine, -minus_sine], axis=1)

    capacities = sorted({max(1, tiles * step // 16) for step in (8, 10, 11, 12, 13, 14, 16)})

    def transform(count, masks, table, sources):
        scratch = (devices, count * SUB, 2 * width)
        outs = [shape(devices, count * halves, 2, SUB, LANES)]
        if masks:
            outs += [
                jax.ShapeDtypeStruct((devices, LANES), jnp.int32),
                jax.ShapeDtypeStruct((devices, LANES), jnp.int32),
                jax.ShapeDtypeStruct((1,), jnp.int32),
            ]
        return call(
            functools.partial(transform_kernel, devices, count, masks),
            outs,
            [VMEM_SPEC] * (2 + len(sources)),
            [
                pltpu.VMEM(scratch, jnp.bfloat16),
                pltpu.VMEM(scratch, jnp.bfloat16),
                pltpu.VMEM(scratch, jnp.float32),
            ],
            cost=pl.CostEstimate(
                flops=6 * devices * count * SUB * 4 * width * width,
                bytes_accessed=16 << 20,
                transcendentals=0,
            ),
        )(table, twiddle, *sources)

    weight = block_weights(block_on, block_band, band_gain, length).reshape(tiles)

    first, index, place, branch = transform(part, (tiles, capacities[:-1]), square(me[0]), arrived)
    own_place = place[devices - 1, :tiles]
    (second,) = transform(blocks - part, (), square(0), [received])

    def finish(capacity):
        def run(me, index, own_place, weight, first, second):
            sent = call(
                functools.partial(compact_kernel, capacity),
                [shape(capacity, 2, SUB, LANES)] * devices,
                [SMEM_SPEC, SMEM_SPEC, VMEM_SPEC, VMEM_SPEC],
            )(me, index, first, second)
            return call(
                functools.partial(spread_kernel, devices),
                shape(*slab.shape),
                [SMEM_SPEC] * 3 + [VMEM_SPEC] * devices,
                [pltpu.VMEM(slab.shape, jnp.float32), pltpu.SemaphoreType.DMA((blocks,))],
                out_spec=HBM_SPEC,
            )(me, own_place, weight, *trade(sent))

        return run

    branches = [finish(c) for c in capacities]
    return branch[0], branches, (me, index, own_place, weight, first, second)


def shards(slab, block_on, block_band, band_gain):
    devices = lax.axis_size("col")
    rows_total, shard_cols = slab.shape[1:]
    power = devices & (devices - 1) == 0
    fits = (
        power
        and 2 <= devices <= 32
        and devices * SUB == BLOCK
        and shard_cols == 2 * LANES
        and rows_total % (4 * BLOCK) == 0
        and rows_total // BLOCK * 2 <= LANES
    )
    if fits:
        branch, branches, operands = shards_tiled(slab, block_on, block_band, band_gain)
        return lax.switch(branch, branches, *operands)
    return shards_generic(slab, block_on, block_band, band_gain)


def solution(mesh):
    placed = (P(None, "groups", "col"), P("groups", "col"), P("groups", "col"), P())
    return jax.shard_map(
        shards, mesh=mesh, in_specs=placed, out_specs=P(None, "groups", "col"), check_vma=False
    )
```

```python
import functools
import math

import jax
import jax.numpy as jnp
from jax import lax
from jax.experimental import pallas as pl
from jax.experimental.pallas import tpu as pltpu
from jax.sharding import PartitionSpec as P


BLOCK = 128
SUB = 8
LANES = 128


def phase_table(first_index, second_index, length):
    product = first_index[:, None] * second_index[None, :] % length
    angles = product.astype(jnp.float32) * (2.0 * math.pi / length)
    return (jnp.cos(angles), -jnp.sin(angles))


def contract(stacked, table, formula):
    cosine_table, sine_table = table
    ein = functools.partial(jnp.einsum, formula, precision=lax.Precision.HIGHEST)
    real_part = ein(stacked[0], cosine_table) - ein(stacked[1], sine_table)
    imag_part = ein(stacked[0], sine_table) + ein(stacked[1], cosine_table)
    return jnp.stack([real_part, imag_part])


def rotate(stacked, table):
    cosine_table, sine_table = table
    real_part = stacked[0] * cosine_table - stacked[1] * sine_table
    imag_part = stacked[0] * sine_table + stacked[1] * cosine_table
    return jnp.stack([real_part, imag_part])


def block_weights(block_on, block_band, band_gain, length):
    choose = (block_band[..., None] == jnp.arange(band_gain.shape[0], dtype=jnp.int32)).astype(
        jnp.float32
    )
    factor = 1.0 / math.sqrt(length)
    return block_on.astype(jnp.float32) * jnp.sum(choose * band_gain, axis=-1) * factor


def shards_generic(slab, block_on, block_band, band_gain):
    devices = lax.axis_size("col")
    rows_total, shard_cols = slab.shape[1:]
    length = shard_cols * devices
    rows_here = rows_total // devices
    first_len = BLOCK
    second_len = length // first_len
    first_iota = jnp.arange(first_len, dtype=jnp.int32)
    second_iota = jnp.arange(second_len, dtype=jnp.int32)
    table_one = phase_table(first_iota, first_iota, first_len)
    table_middle = phase_table(first_iota, second_iota, length)
    table_two = phase_table(second_iota, second_iota, second_len)
    received = lax.all_to_all(
        slab.reshape(2, devices, rows_here, shard_cols), "col", split_axis=1, concat_axis=3, tiled=True
    )
    square = received[:, 0].reshape(2, rows_here, first_len, second_len)
    mixture = rotate(contract(square, table_one, "rab,ak->rkb"), table_middle)
    whole = contract(mixture, table_two, "rkb,bm->rmk").reshape(2, rows_here, devices, shard_cols)
    spectrum = lax.all_to_all(whole, "col", split_axis=2, concat_axis=1, tiled=True)
    weight = block_weights(block_on, block_band, band_gain, length)
    blocked = spectrum.reshape(2, rows_total // BLOCK, BLOCK, shard_cols // BLOCK, BLOCK)
    return (blocked * weight[None, :, None, :, None]).reshape(2, rows_total, shard_cols)


def travel_order(devices):
    return sorted(range(devices), key=lambda hop: (-hop.bit_length(), hop))


def pack_all_kernel(first, blocks, slab_ref, out_ref, sem):
    halves = slab_ref.shape[4] // LANES
    copies = []
    for plane in range(2):
        for block in range(blocks):
            for half in range(halves):
                copies.append(
                    pltpu.make_async_copy(
                        slab_ref.at[plane, first + block, :, :, half * LANES : (half + 1) * LANES],
                        out_ref.at[:, (plane * halves + half) * blocks + block],
                        sem.at[len(copies)],
                    )
                )
    for copy in copies:
        copy.start()
    for copy in copies:
        copy.wait()


def pack_each_kernel(first, blocks, me_ref, slab_ref, mask_ref, *refs):
    outs, sem = refs[:-1], refs[-1]
    halves = slab_ref.shape[4] // LANES
    me = me_ref[0]
    copies = []
    for hop, out in zip(travel_order(len(outs)), outs):
        for plane in range(2):
            for half in range(halves):
                tile = (plane * halves + half) * blocks
                lanes = slice(half * LANES, (half + 1) * LANES)
                copies.append(
                    pltpu.make_async_copy(
                        slab_ref.at[plane, first : first + blocks, me ^ hop, :, lanes],
                        out.at[tile : tile + blocks],
                        sem.at[len(copies)],
                    )
                )
        copies.append(
            pltpu.make_async_copy(mask_ref, out.at[2 * halves * blocks], sem.at[len(copies)])
        )
    for copy in copies:
        copy.start()
    for copy in copies:
        copy.wait()


def butterflies(parts, length):
    if length == 1:
        return parts
    even = butterflies(parts[0::2], length // 2)
    odd = butterflies(parts[1::2], length // 2)
    low, high = [], []
    for index in range(length // 2):
        even_re, even_im = even[index]
        odd_re, odd_im = odd[index]
        if index == 0:
            turn_re, turn_im = odd_re, odd_im
        elif 4 * index == length:
            turn_re, turn_im = odd_im, -odd_re
        elif 8 * index == length:
            root = math.sqrt(0.5)
            turn_re, turn_im = (odd_re + odd_im) * root, (odd_im - odd_re) * root
        elif 8 * index == 3 * length:
            root = math.sqrt(0.5)
            turn_re, turn_im = (odd_im - odd_re) * root, (odd_re + odd_im) * -root
        else:
            angle = 2.0 * math.pi * index / length
            cosine, sine = math.cos(angle), math.sin(angle)
            turn_re = odd_re * cosine + odd_im * sine
            turn_im = odd_im * cosine - odd_re * sine
        low.append((even_re + turn_re, even_im + turn_im))
        high.append((even_re - turn_re, even_im - turn_im))
    return low + high


def slots_kernel(tiles, bounds, sources, index_ref, place_ref, branch_ref):
    count = len(sources)
    flags = jnp.concatenate([source[source.shape[0] - 1, 0:1] for source in sources], axis=0)
    live = flags > 0.5
    lane = lax.broadcasted_iota(jnp.int32, (count, LANES), 1)
    row = lax.broadcasted_iota(jnp.int32, (LANES, LANES), 0)
    column = lax.broadcasted_iota(jnp.int32, (LANES, LANES), 1)
    ones = jnp.where(live, 1.0, 0.0)
    rank = jnp.dot(
        ones.astype(jnp.bfloat16),
        jnp.where(row < column, 1.0, 0.0).astype(jnp.bfloat16),
        preferred_element_type=jnp.float32,
    ).astype(jnp.int32)
    place = jnp.where(live, rank, LANES)
    index = jnp.zeros((count, LANES), jnp.int32)
    for tile in range(tiles):
        index = jnp.where(place[:, tile : tile + 1] == lane, tile, index)
    index_ref[...] = index
    place_ref[...] = rank
    most = jnp.max(jnp.sum(ones, axis=1, keepdims=True)).astype(jnp.int32)
    branch_ref[0] = sum((most > bound).astype(jnp.int32) for bound in bounds)


def transform_kernel(devices, blocks, masks, table_ref, twiddle_ref, *refs):
    sources, (high_ref, low_ref, mid_ref) = refs[: -7 if masks else -4], refs[-3:]
    out_ref = refs[len(sources)]
    if masks:
        slots_kernel(*masks, sources, *refs[len(sources) + 1 : len(sources) + 4])
    halves = 2
    width = halves * LANES
    bits = devices.bit_length() - 1
    lane = lax.broadcasted_iota(jnp.int32, (2 * SUB, LANES), 1)

    place = travel_order(devices)

    def tile_of(dev, plane, block, half):
        if len(sources) == 1:
            return sources[0][dev, (plane * halves + half) * blocks + block]
        return sources[place.index(dev)][(plane * halves + half) * blocks + block]

    @pl.loop(0, blocks // 2)
    def _(pair):
        for plane in range(2):
            for half in range(halves):
                vals = [
                    jnp.concatenate(
                        [
                            tile_of(dev, plane, pair * 2, half),
                            tile_of(dev, plane, pair * 2 + 1, half),
                        ],
                        axis=0,
                    )
                    for dev in range(devices)
                ]
                for bit in range(bits):
                    step = 1 << bit
                    odd_lane = (lane & step) != 0
                    for dev in range(devices):
                        if dev & step:
                            continue
                        first, second = vals[dev], vals[dev | step]
                        moved = jnp.take_along_axis(
                            jnp.where(odd_lane, first, second), lane ^ step, axis=1
                        )
                        vals[dev] = jnp.where(odd_lane, moved, first)
                        vals[dev | step] = jnp.where(odd_lane, second, moved)
                where = slice(plane * width + half * LANES, plane * width + (half + 1) * LANES)
                for dev in range(devices):
                    high = vals[dev].astype(jnp.bfloat16)
                    low = (vals[dev] - high.astype(jnp.float32)).astype(jnp.bfloat16)
                    high_ref[dev, pl.ds(pair * 2 * SUB, 2 * SUB), where] = high
                    low_ref[dev, pl.ds(pair * 2 * SUB, 2 * SUB), where] = low

    rows = blocks * SUB
    dot = functools.partial(jnp.dot, preferred_element_type=jnp.float32)
    lhs_high = high_ref[...].reshape(devices * rows, 2 * width)
    lhs_low = low_ref[...].reshape(devices * rows, 2 * width)
    for plane in range(2):
        columns = slice(plane * width, (plane + 1) * width)
        table = table_ref[:, columns]
        table_high = table.astype(jnp.bfloat16)
        table_low = (table - table_high.astype(jnp.float32)).astype(jnp.bfloat16)
        total = dot(lhs_high, table_high) + (dot(lhs_high, table_low) + dot(lhs_low, table_high))
        mid_ref[:, :, columns] = total.reshape(devices, rows, width)

    @pl.loop(0, blocks)
    def _(block):
        for half in range(halves):
            parts = []
            for dev in range(devices):
                re = mid_ref[dev, pl.ds(block * SUB, SUB), half * LANES : (half + 1) * LANES]
                im = mid_ref[
                    dev, pl.ds(block * SUB, SUB), width + half * LANES : width + (half + 1) * LANES
                ]
                if dev:
                    cosine = twiddle_ref[dev : dev + 1, half * LANES : (half + 1) * LANES]
                    sine = twiddle_ref[dev : dev + 1, width + half * LANES : width + (half + 1) * LANES]
                    re, im = re * cosine + im * sine, im * cosine - re * sine
                parts.append((re, im))
            for dev, (re, im) in enumerate(butterflies(parts, devices)):
                out_ref[dev, block * halves + half, 0] = re
                out_ref[dev, block * halves + half, 1] = im


def compact_kernel(devices, slots, numbers, me_ref, index_ref, first_ref, second_ref, *outs):
    split = first_ref.shape[1]
    me = me_ref[0]
    order = travel_order(devices)
    for number, out in zip(numbers, outs):
        dev = me ^ order[number]
        for slot in range(slots):
            index = index_ref[number, slot]
            early = first_ref[dev, jnp.minimum(index, split - 1)]
            late = second_ref[dev, jnp.maximum(index - split, 0)]
            out[slot] = jnp.where(index < split, early, late)


def spread_kernel(devices, me_ref, slot_ref, weight_ref, *refs):
    sources, (out_ref, stage_ref, sem) = refs[:-3], refs[-3:]
    halves = out_ref.shape[2] // LANES
    blocks = out_ref.shape[1] // BLOCK
    last = sources[0].shape[0] - 1
    me = me_ref[0]

    def copy_of(block):
        rows = pl.ds(pl.multiple_of(block * BLOCK, BLOCK), BLOCK)
        return pltpu.make_async_copy(stage_ref.at[:, rows], out_ref.at[:, rows], sem.at[block])

    @pl.loop(0, blocks)
    def _(block):
        for half in range(halves):
            slot = jnp.minimum(slot_ref[block * halves + half], last)
            weight = weight_ref[block * halves + half]
            for number, hop in enumerate(travel_order(devices)):
                row = pl.multiple_of(block * BLOCK + (me ^ hop) * SUB, SUB)
                for plane in range(2):
                    stage_ref[plane, pl.ds(row, SUB), half * LANES : (half + 1) * LANES] = (
                        sources[number][slot, plane] * weight
                    )
        copy_of(block).start()

    @pl.loop(0, blocks)
    def _(block):
        copy_of(block).wait()


VMEM_SPEC = pl.BlockSpec(memory_space=pltpu.VMEM)
SMEM_SPEC = pl.BlockSpec(memory_space=pltpu.SMEM)
ANY_SPEC = pl.BlockSpec(memory_space=pl.ANY)
HBM_SPEC = pl.BlockSpec(memory_space=pltpu.HBM)
PIECE_SPEC = HBM_SPEC


def shards_tiled(slab, block_on, block_band, band_gain):
    devices = lax.axis_size("col")
    rows_total, shard_cols = slab.shape[1:]
    length = shard_cols * devices
    blocks = rows_total // BLOCK
    halves = shard_cols // LANES
    tiles = blocks * halves
    width = shard_cols
    part = blocks * 3 // 4
    early = part * halves
    me = lax.axis_index("col").astype(jnp.int32).reshape(1)

    def call(body, out_shape, in_specs, scratch=(), cost=None, out_spec=VMEM_SPEC, mib=14):
        many = isinstance(out_shape, list)
        return pl.pallas_call(
            body,
            out_shape=out_shape,
            in_specs=in_specs,
            out_specs=[
                SMEM_SPEC if out.shape == (1,) else out_spec for out in out_shape
            ]
            if many
            else out_spec,
            scratch_shapes=scratch,
            compiler_params=pltpu.CompilerParams(vmem_limit_bytes=mib << 20),
            cost_estimate=cost,
        )

    def trade(values, numbers=range(devices)):
        traded = []
        for number, value in zip(numbers, values):
            hop = travel_order(devices)[number]
            pairs = [(dev, dev ^ hop) for dev in range(devices)]
            traded.append(lax.ppermute(value, "col", pairs) if hop else value)
        return traded

    def shape(*dims):
        return jax.ShapeDtypeStruct(dims, jnp.float32)

    dealt = slab.reshape(2, blocks, devices, SUB, shard_cols)
    flags = jnp.zeros((SUB, LANES), jnp.float32)
    flags = flags.at[0, :tiles].set(block_on.reshape(tiles).astype(jnp.float32))
    pieces = call(
        functools.partial(pack_each_kernel, 0, part),
        [shape(2 * early + 1, SUB, LANES)] * devices,
        [SMEM_SPEC, VMEM_SPEC, VMEM_SPEC],
        [pltpu.SemaphoreType.DMA((devices * (2 * halves + 1),))],
        out_spec=PIECE_SPEC,
    )(me, dealt, flags)
    arrived = trade(pieces)
    message = call(
        functools.partial(pack_all_kernel, part, blocks - part),
        shape(devices, 2 * (tiles - early), SUB, LANES),
        [VMEM_SPEC],
        [pltpu.SemaphoreType.DMA((2 * (tiles - early),))],
    )(dealt)
    received = lax.all_to_all(message, "col", split_axis=0, concat_axis=0, tiled=True)

    lane = jnp.arange(width, dtype=jnp.int32)

    def square(shift):
        point = ((lane % devices) ^ shift) * (width // devices) + lane // devices
        cosine, minus_sine = phase_table(point, lane, width)
        return jnp.concatenate(
            [
                jnp.concatenate([cosine, minus_sine], axis=1),
                jnp.concatenate([-minus_sine, cosine], axis=1),
            ],
            axis=0,
        )

    cosine, minus_sine = phase_table(jnp.arange(devices, dtype=jnp.int32), lane, length)
    twiddle = jnp.concatenate([cosine, -minus_sine], axis=1)

    capacities = sorted({max(1, tiles * step // 16) for step in (8, 10, 11, 12, 13, 14, 16)})

    def transform(count, masks, table, sources):
        scratch = (devices, count * SUB, 2 * width)
        outs = [shape(devices, count * halves, 2, SUB, LANES)]
        if masks:
            outs += [
                jax.ShapeDtypeStruct((devices, LANES), jnp.int32),
                jax.ShapeDtypeStruct((devices, LANES), jnp.int32),
                jax.ShapeDtypeStruct((1,), jnp.int32),
            ]
        return call(
            functools.partial(transform_kernel, devices, count, masks),
            outs,
            [VMEM_SPEC] * (2 + len(sources)),
            [
                pltpu.VMEM(scratch, jnp.bfloat16),
                pltpu.VMEM(scratch, jnp.bfloat16),
                pltpu.VMEM(scratch, jnp.float32),
            ],
            cost=pl.CostEstimate(
                flops=6 * devices * count * SUB * 4 * width * width,
                bytes_accessed=16 << 20,
                transcendentals=0,
            ),
        )(table, twiddle, *sources)

    weight = block_weights(block_on, block_band, band_gain, length).reshape(tiles)

    first, index, place, branch = transform(part, (tiles, capacities[:-1]), square(me[0]), arrived)
    own_place = place[devices - 1, :tiles]
    (second,) = transform(blocks - part, (), square(0), [received])

    def finish(capacity):
        def run(me, index, own_place, weight, first, second):
            sent = []
            for numbers in (range(4), range(4, devices)):
                packed = call(
                    functools.partial(compact_kernel, devices, capacity, list(numbers)),
                    [shape(capacity, 2, SUB, LANES)] * len(numbers),
                    [SMEM_SPEC, SMEM_SPEC, VMEM_SPEC, VMEM_SPEC],
                )(me, index, first, second)
                sent += trade(packed, numbers)
            return call(
                functools.partial(spread_kernel, devices),
                shape(*slab.shape),
                [SMEM_SPEC] * 3 + [VMEM_SPEC] * devices,
                [pltpu.VMEM(slab.shape, jnp.float32), pltpu.SemaphoreType.DMA((blocks,))],
                out_spec=HBM_SPEC,
            )(me, own_place, weight, *sent)

        return run

    branches = [finish(c) for c in capacities]
    return branch[0], branches, (me, index, own_place, weight, first, second)


def shards(slab, block_on, block_band, band_gain):
    devices = lax.axis_size("col")
    rows_total, shard_cols = slab.shape[1:]
    power = devices & (devices - 1) == 0
    fits = (
        power
        and 2 <= devices <= 32
        and devices * SUB == BLOCK
        and shard_cols == 2 * LANES
        and rows_total % (4 * BLOCK) == 0
        and rows_total // BLOCK * 2 <= LANES
    )
    if fits:
        branch, branches, operands = shards_tiled(slab, block_on, block_band, band_gain)
        return lax.switch(branch, branches, *operands)
    return shards_generic(slab, block_on, block_band, band_gain)


def solution(mesh):
    placed = (P(None, "groups", "col"), P("groups", "col"), P("groups", "col"), P())
    return jax.shard_map(
        shards, mesh=mesh, in_specs=placed, out_specs=P(None, "groups", "col"), check_vma=False
    )
```
